32 devices in a mesh: wide: 8 (over z, x), narrow: 4 (over y, core).
Axes of the slice: x: 2, y: 2, z: 4, core: 2. Of those that a mesh axis runs over, the one named last changes fastest.
Arguments:
- samples: bfloat16 [16384, 1024], P(('wide', 'narrow')), may hold values from -16 to 16
- centroid_table: bfloat16 [16384, 1024], P('wide', 'narrow'), may hold values from -6 to 6
- owner: int32 [16384], replicated, may hold values from 0 to 7, as said below
- slot: int32 [16384], replicated, may hold values from 0 to 2047, as said below
- assign: int32 [16384], P('wide'), may hold values from 0 to 16383, as said below
- codebook: float32 [8, 2048, 128], P('narrow'), may hold values from -16 to 16
Outputs:
- residual: bfloat16 [16384, 1024], P('wide', 'narrow')
- refined: float32 [8, 2048, 128], P('narrow')
The draws below stay inside these ranges and needn't reach their ends.
Inputs may be any that keep to these rules, and one draw needn't show every extreme that they name: owner and slot give each coarse centroid a distinct storage position owner * 2048 + slot. `slot`: see owner. `assign`: in each aligned block of 2048 rows (the rows of one index of wide), at most 512 rows have centroids with one owner, and some owner has exactly 512.
All inputs are finite; a program needn't handle non-finite values.
Results may differ from the reference program's by a relative error of at most 0.0079.
Values may be sent and summed in bfloat16 or wider, within the bound.
No kernel may reach another device: no remote copies, remote signals or barrier semaphores. Data moves between devices by JAX's collectives and lax.ppermute only.
A program may use at most 64 MiB of HBM per device.

```python
import jax
import jax.numpy as jnp
from jax import lax

D = 1024
SUB = 128
K = 2048
SLOTS = 2048
ITERS = 2
M = 8
NLIST = 16384
GROUP = 2048
ROWS = 16384
CAP = 512


def placed_order(key):
    return jax.random.permutation(jax.random.fold_in(key, 11), NLIST).astype(jnp.int32)


def draw_owner(key, part):
    position = jnp.argsort(placed_order(key))
    return (position // SLOTS).astype(jnp.int32)


def draw_slot(key, part):
    position = jnp.argsort(placed_order(key))
    return (position % SLOTS).astype(jnp.int32)


def draw_assign(key, part):
    placed = placed_order(key)
    occupant_sequence = NLIST // SLOTS
    place_sequence = occupant_sequence * CAP

    def draw_group(cluster_draw_seed):
        frequent_draw_seed, extra_credit_seed, chair_draw_seed, blend_draw_seed, bucket_draw_seed = jax.random.split(cluster_draw_seed, 5)
        hottest = jax.random.randint(frequent_draw_seed, (), 0, occupant_sequence)
        occupant_extra_credit = jax.random.randint(extra_credit_seed, (occupant_sequence,), 0, 1024)
        place_occupant = jnp.arange(place_sequence, dtype=jnp.int32) // CAP
        place_merit = jax.random.randint(chair_draw_seed, (place_sequence,), 0, 1024) + occupant_extra_credit[place_occupant]
        place_merit = place_merit + (place_occupant == hottest).astype(jnp.int32) * 4096
        place_merit = place_merit * place_sequence + jnp.arange(place_sequence, dtype=jnp.int32)
        ranking = jnp.argsort(-place_merit)
        row_owner = place_occupant[ranking[:GROUP]]
        row_owner = row_owner[jax.random.permutation(blend_draw_seed, GROUP)]
        row_slot = jax.random.randint(bucket_draw_seed, (GROUP,), 0, SLOTS)
        return placed[row_owner * SLOTS + row_slot]
    group_keys = jax.random.split(jax.random.fold_in(key, 23), ROWS // GROUP)
    return jax.vmap(draw_group)(group_keys).reshape(ROWS).astype(jnp.int32)


def draw_codebook(key, part):
    key_base = jax.random.fold_in(jax.random.fold_in(key, 31), 0)
    base = jax.random.normal(key_base, (M, K, SUB), jnp.float32)
    return jnp.clip(base, -16.0, 16.0)


def draw_samples(key, part):
    key_base = jax.random.fold_in(jax.random.fold_in(key, 41), 0)
    base = jax.random.normal(key_base, (ROWS, D), jnp.float32)
    return jnp.clip(base, -16.0, 16.0).astype(jnp.bfloat16)


def shard_levels(rng, dims, cuts, least, largest):
    def one(dim, blocks):
        heights = jax.random.uniform(jax.random.fold_in(jax.random.fold_in(rng, 6), dim), (blocks,), jnp.float32, least / len(cuts), largest / len(cuts))
        return jnp.repeat(jnp.exp(heights), dims[dim] // blocks).reshape((-1,) + (1,) * (len(dims) - dim - 1))

    factor_of = one(*cuts[0])
    for cut in cuts[1:]:
        factor_of = factor_of * one(*cut)
    return factor_of


def scatter_about(key, extent, scale, most, cuts=(), kind=jnp.bfloat16):
    level = shard_levels(key, extent, cuts, -0.22, 0.18) if cuts else 1.0
    entries = jax.random.normal(key, extent, jnp.float32) * scale * level
    return jnp.minimum(jnp.maximum(entries, -most), most).astype(kind)


def setup_inputs(seed: int = 0) -> dict:
    keys = jax.random.split(jax.random.key(seed), 7)
    samples = draw_samples(jax.random.fold_in(keys[6], 71), 0)
    centroid_table = scatter_about(keys[1], (NLIST, D), 1.0, 6.0, ((0, 8), (1, 4)))
    owner = draw_owner(jax.random.fold_in(keys[6], 71), 0)
    slot = draw_slot(jax.random.fold_in(keys[6], 71), 0)
    assign = draw_assign(jax.random.fold_in(keys[6], 71), 0)
    codebook = draw_codebook(jax.random.fold_in(keys[6], 71), 0)
    return dict(samples=samples, centroid_table=centroid_table, owner=owner, slot=slot, assign=assign, codebook=codebook)


softness_level = 16.0
prior_weight = 1.0


def refine(space_rows, codewords):
    blocks = space_rows.reshape(ROWS // GROUP, GROUP, SUB)
    for iteration in range(ITERS):
        narrow_words = lax.optimization_barrier(codewords.astype(jnp.bfloat16)).astype(jnp.float32)
        codeword_norm_values = jnp.sum(codewords * codewords, axis=1)

        def block_step(running, row_block):
            values = row_block.astype(jnp.float32)
            inner_product_rows = jnp.dot(values, narrow_words.T, precision=lax.Precision.HIGHEST)
            score_matrix = (2.0 * inner_product_rows - codeword_norm_values[None, :]) / softness_level
            weights_soft = jax.nn.softmax(score_matrix, axis=1)
            rounded = lax.optimization_barrier(weights_soft.astype(jnp.bfloat16)).astype(jnp.float32)
            totals = running[0] + jnp.dot(rounded.T, values, precision=lax.Precision.HIGHEST)
            return (totals, running[1] + jnp.sum(rounded, axis=0)), None

        start = (jnp.zeros((K, SUB), jnp.float32), jnp.zeros((K,), jnp.float32))
        (totals, counts), ignored = lax.scan(block_step, start, blocks)
        codewords = (totals + prior_weight * codewords) / (counts[:, None] + prior_weight)
    return codewords


def reference(samples, centroid_table, owner, slot, assign, codebook):
    position = (owner[assign] * SLOTS + slot[assign]).astype(jnp.int32)
    centre = jnp.take(centroid_table, position, axis=0)
    residual = (samples.astype(jnp.float32) - centre.astype(jnp.float32)).astype(jnp.bfloat16)
    spaces = residual.reshape(ROWS, D // SUB, SUB).transpose(1, 0, 2)
    refined = lax.map(lambda inputs: refine(inputs[0], inputs[1]), (spaces, codebook))
    return residual, refined
```

```python
import functools

import jax
import jax.numpy as jnp
from jax import lax
from jax.experimental import pallas as pl
from jax.experimental.pallas import tpu as pltpu
from jax.sharding import PartitionSpec as P

ITERS = 2
SOFTNESS = 16.0
PRIOR = 1.0
LANES = 128
LOG2E = 1.4426950408889634
TINY = 2.0**-64

f32 = jnp.float32
bf16 = jnp.bfloat16
i32 = jnp.int32

NN = (((1,), (0,)), ((), ()))
NT = (((1,), (1,)), ((), ()))


def mm(a, b, dims=NN):
    return lax.dot_general(a, b, dims, preferred_element_type=f32)


def iota(shape, dim):
    return lax.broadcasted_iota(i32, shape, dim)


def onehot(mask):
    return jnp.where(mask, 1.0, 0.0).astype(bf16)


def pad_rows(x, rows):
    if x.shape[0] == rows:
        return x
    return jnp.concatenate([x, jnp.zeros((rows - x.shape[0],) + x.shape[1:], x.dtype)], axis=0)


def pieces(v):
    high = v.astype(bf16).astype(f32)
    rest = v - high
    middle = rest.astype(bf16).astype(f32)
    return high, middle, rest - middle


def call(body, out_shape, scratch=(), in_specs=None, name=None, prefetch=0):
    return pl.pallas_call(
        body,
        out_shape=out_shape,
        grid_spec=pltpu.PrefetchScalarGridSpec(
            num_scalar_prefetch=prefetch,
            grid=(1,),
            in_specs=in_specs,
            out_specs=jax.tree.map(
                lambda s: pl.BlockSpec(s.shape, lambda i, *_, n=len(s.shape): (0,) * n), out_shape
            ),
            scratch_shapes=scratch,
        ),
        compiler_params=pltpu.CompilerParams(vmem_limit_bytes=56 * 1024 * 1024),
        name=name,
    )


def whole(x):
    return pl.BlockSpec(x.shape, lambda i, *_, n=len(x.shape): (0,) * n)


def lookup_kernel(wide, cap, assign_ref, owner_ref, slot_ref, req_ref, own_ref, rank_ref, hot, looked, stack, weighted, ranked):
    blocks = assign_ref.shape[0]
    high_count = owner_ref.shape[0]
    group = stack.shape[0] // blocks
    assign = assign_ref[...]
    high = assign >> 7
    low = assign & (LANES - 1)
    sub_high = iota((high_count, LANES), 0)
    for c in range(blocks):
        hot[:, c * LANES : (c + 1) * LANES] = onehot(sub_high == high[c : c + 1, :])
    slots = slot_ref[...]
    table = jnp.concatenate(
        [t.astype(f32).T for t in (owner_ref[...], slots >> 8, slots & 255)], axis=0
    ).astype(bf16)
    looked[...] = mm(table, hot[...])
    sub = iota((LANES, LANES), 0)
    sub_group = iota((group, LANES), 0).astype(f32)
    for c in range(blocks):
        lanes = slice(c * LANES, (c + 1) * LANES)
        pick = sub == low[c : c + 1, :]
        values = [
            jnp.sum(jnp.where(pick, looked[p * LANES : (p + 1) * LANES, lanes], 0.0), axis=0, keepdims=True)
            for p in range(3)
        ]
        mine = jnp.where(sub_group == values[0], 1.0, 0.0)
        own_ref[c : c + 1, :] = values[0].astype(i32)
        stack[c * group : (c + 1) * group, :] = mine.astype(bf16)
        weighted[0:group, lanes] = (mine * values[1]).astype(bf16)
        weighted[group : 2 * group, lanes] = (mine * values[2]).astype(bf16)
    before = onehot(iota((LANES, LANES), 0) < iota((LANES, LANES), 1))
    inside = mm(stack[...], before)
    count = mm(stack[...], jnp.ones((LANES, LANES), bf16))
    offset = jnp.zeros((group, LANES), f32)
    sub_cap = iota((cap, LANES), 0).astype(f32)
    for c in range(blocks):
        rows = slice(c * group, (c + 1) * group)
        mine = stack[rows, :].astype(f32)
        rank = jnp.sum(mine * (inside[rows, :] + offset), axis=0, keepdims=True)
        offset = offset + count[rows, :]
        rank_ref[c : c + 1, :] = rank.astype(i32)
        ranked[:, c * LANES : (c + 1) * LANES] = onehot(sub_cap == rank)
    found = mm(weighted[...], ranked[...], NT)
    req_ref[...] = (found[0:wide] * 256.0 + found[group : group + wide]).astype(i32)


def lookup(assign, owner, slot, wide, cap):
    rows = assign.shape[0]
    blocks = rows // LANES
    high_count = owner.shape[0] // LANES
    group = max(wide, 16)
    args = (
        assign.reshape(blocks, LANES),
        owner.reshape(high_count, LANES),
        slot.reshape(high_count, LANES),
    )
    return call(
        functools.partial(lookup_kernel, wide, cap),
        (
            jax.ShapeDtypeStruct((wide, cap), i32),
            jax.ShapeDtypeStruct((blocks, LANES), i32),
            jax.ShapeDtypeStruct((blocks, LANES), i32),
        ),
        scratch=[
            pltpu.VMEM((high_count, rows), bf16),
            pltpu.VMEM((3 * LANES, rows), f32),
            pltpu.VMEM((blocks * group, LANES), bf16),
            pltpu.VMEM((2 * group, rows), bf16),
            pltpu.VMEM((cap, rows), bf16),
        ],
        in_specs=[whole(a) for a in args],
        name="lookup",
    )(*args)


def pick_kernel(spaces, step, req_ref, table_ref, *outs):
    wide, cap = req_ref.shape
    slots = table_ref.shape[0]
    req = pad_rows(req_ref[...], LANES)
    shift = step.bit_length() - 1
    high_t = (req >> shift).astype(f32).T
    low_t = (req & (step - 1)).astype(f32).T
    lane = iota((cap, step), 1).astype(f32)
    for d in range(wide):
        hot = onehot(lane == low_t[:, d : d + 1])
        high = high_t[:, d : d + 1]
        rows = mm(hot, table_ref[0:step, :])
        for h in range(1, slots // step):
            rows = jnp.where(high == float(h), mm(hot, table_ref[h * step : (h + 1) * step, :]), rows)
        for i in range(spaces):
            block = (d % spaces + 1 + i) % spaces
            outs[i][d] = rows[:, block * LANES : (block + 1) * LANES].astype(bf16)


def pick(req, table, spaces):
    wide, cap = req.shape
    return call(
        functools.partial(pick_kernel, spaces, min(512, table.shape[0])),
        tuple(jax.ShapeDtypeStruct((wide, cap, LANES), bf16) for _ in range(spaces)),
        in_specs=[whole(req), whole(table)],
        name="pick",
    )(req, table)


def place_kernel(wide, where_ref, own_ref, rank_ref, sample_ref, *refs):
    bufs, (res_ref, res_t_ref) = refs[:wide], refs[wide:]
    rows = sample_ref.shape[0]
    cap = bufs[0].shape[0]
    me = where_ref[0]
    own_t = pad_rows(own_ref[...], LANES).astype(f32).T
    rank_t = pad_rows(rank_ref[...], LANES).astype(f32).T
    lane = iota((LANES, cap), 1).astype(f32)
    for b in range(rows // LANES):
        hot = onehot(lane == rank_t[:, b : b + 1])
        owner = own_t[:, b : b + 1]
        total = jnp.zeros((LANES, LANES), f32)
        for k in range(0, wide, 2):
            pair = mm(hot, jnp.concatenate([bufs[k][...], bufs[k + 1][...]], axis=1))
            for t in range(2):
                source = (me ^ (k + t)).astype(f32)
                total = jnp.where(owner == source, pair[:, t * LANES : (t + 1) * LANES], total)
        part = slice(b * LANES, (b + 1) * LANES)
        res = (sample_ref[part, :].astype(f32) - total).astype(bf16)
        res_ref[part, :] = res
        res_t_ref[:, part] = res.astype(f32).T.astype(bf16)


def place(me, column, own, rank, samples, bufs):
    wide = len(bufs)
    rows = samples.shape[0]
    where = jnp.stack([me, column]).astype(i32)
    return call(
        functools.partial(place_kernel, wide),
        (
            jax.ShapeDtypeStruct((rows, LANES), bf16),
            jax.ShapeDtypeStruct((LANES, rows), bf16),
        ),
        in_specs=[whole(own), whole(rank), pl.BlockSpec((rows, LANES), lambda i, w: (0, w[1]))]
        + [whole(b) for b in bufs],
        name="place",
        prefetch=1,
    )(where, own, rank, samples, *bufs)


def words_block(words, norm_columns):
    rows = words.shape[0]
    lane = iota((rows, LANES), 1)
    extra = jnp.where((lane >= 3) & (lane < 6), 1.0, 0.0)
    for p in range(3):
        extra = jnp.where(lane == p, norm_columns[p], extra)
    return jnp.concatenate([words * (2.0 / SOFTNESS), extra], axis=1).astype(bf16)


def first_words_kernel(where_ref, code_ref, words_ref):
    count = code_ref.shape[1]
    step = min(256, count)
    for b in range(count // step):
        part = slice(b * step, (b + 1) * step)
        code = code_ref[0, part, :]
        norm = jnp.sum(code * code, axis=1, keepdims=True) * (-1.0 / SOFTNESS)
        words_ref[part, :] = words_block(code.astype(bf16).astype(f32), pieces(norm))


def first_words(space, codebook):
    _, count, width = codebook.shape
    return call(
        first_words_kernel,
        jax.ShapeDtypeStruct((count, 2 * LANES), bf16),
        in_specs=[pl.BlockSpec((1, count, width), lambda i, w: (w[0], 0, 0))],
        name="first_words",
        prefetch=1,
    )(space.reshape(1).astype(i32), codebook)


def next_words_kernel(shard, where_ref, *refs):
    messages, words_ref = refs[:-1], refs[-1]
    q = where_ref[0]
    size = min(shard, LANES)
    per = shard // size
    for k, ref in enumerate(messages):
        norm_t = pad_rows(ref[shard:, :].astype(f32), LANES).T
        first = (q ^ k) * shard
        for a in range(per):
            columns = [norm_t[0:size, p * per + a : p * per + a + 1] for p in range(3)]
            words = ref[a * size : (a + 1) * size, :].astype(f32)
            start = pl.multiple_of(first + a * size, size)
            words_ref[pl.ds(start, size), :] = words_block(words, columns)


def next_words(q, messages, shard):
    return call(
        functools.partial(next_words_kernel, shard),
        jax.ShapeDtypeStruct((shard * len(messages), 2 * LANES), bf16),
        in_specs=[whole(m) for m in messages],
        name="next_words",
        prefetch=1,
    )(q.reshape(1).astype(i32), *messages)


def pass_kernel(parts, shards, block, words_ref, *refs):
    inputs, out_ref, aug, soft, scaled, least = refs[:parts], *refs[parts:]
    words = words_ref.shape[0]
    rows = inputs[0].shape[1]
    step = min(256, words)
    sub = iota((16, block), 0)
    sub_wide = iota((LANES, block), 0)

    def softmax_block(b, slow):
        lanes = pl.ds(pl.multiple_of(b * block, block), block)
        points = aug[:, lanes]

        def scores(c):
            return mm(words_ref[c * step : (c + 1) * step, :], points)

        top = None
        if slow:
            for c in range(words // step):
                now = jnp.max(scores(c), axis=0, keepdims=True)
                top = now if top is None else jnp.maximum(top, now)
        total = jnp.zeros((8, block), f32)
        for c in range(words // step):
            s = scores(c)
            if slow:
                s = s - top
            e = jnp.exp2(s * LOG2E)
            total = total + jnp.sum(e.reshape(step // 8, 8, block), axis=0)
            soft[c * step : (c + 1) * step, lanes] = e.astype(bf16)
        total = jnp.sum(total, axis=0, keepdims=True)
        inverse = 1.0 / total
        x = points[0:LANES, :].astype(f32)
        high = inverse.astype(bf16).astype(f32)
        tail = jnp.where(sub_wide == 0, high, jnp.where(sub_wide == 1, inverse - high, 0.0))
        both = jnp.concatenate([x * inverse, tail], axis=0)
        scaled[lanes, :] = both.T.astype(bf16)
        return total

    for n, ref in enumerate(inputs):
        for b in range(rows // block):
            part = slice(b * block, (b + 1) * block)
            lanes = slice(n * rows + b * block, n * rows + (b + 1) * block)
            x = ref[:, part]
            wide_x = x.astype(f32)
            norm = jnp.sum(wide_x * wide_x, axis=0, keepdims=True) * (-1.0 / SOFTNESS)
            head = jnp.where(sub < 3, 1.0, 0.0)
            for p, piece in enumerate(pieces(norm)):
                head = jnp.where(sub == 3 + p, piece, head)
            aug[0:LANES, lanes] = x
            aug[LANES : LANES + 16, lanes] = head.astype(bf16)
            aug[LANES + 16 :, lanes] = jnp.zeros((LANES - 16, block), bf16)
    count = parts * rows // block
    least[...] = jnp.full(least.shape, 1.0, f32)

    def fast(b, carry):
        total = softmax_block(b, False)
        least[...] = jnp.minimum(least[...], total)
        return carry

    lax.fori_loop(0, count, fast, 0)

    @pl.when(jnp.min(least[...]) < TINY)
    def _():
        def exact(b, carry):
            softmax_block(b, True)
            return carry

        lax.fori_loop(0, count, exact, 0)

    shard = words // shards
    size = min(shard, LANES)
    per = shard // size
    extra = out_ref.shape[1] - shard
    lane_row = iota((extra, LANES), 0)
    for j in range(shards):
        tail = jnp.zeros((extra, LANES), f32)
        sums = mm(soft[j * shard : (j + 1) * shard, :], scaled[...])
        out_ref[j, 0:shard, :] = sums[:, 0:LANES].astype(bf16)
        for a in range(per):
            turned = pad_rows(sums[a * size : (a + 1) * size, LANES:], LANES).T
            counts = turned[0:1, :] + turned[1:2, :]
            high = counts.astype(bf16).astype(f32)
            tail = jnp.where(lane_row == a, high, tail)
            tail = jnp.where(lane_row == per + a, counts - high, tail)
        out_ref[j, shard:, :] = tail.astype(bf16)


def em_pass(words, inputs, shards, extra):
    count = words.shape[0]
    rows = inputs[0].shape[1]
    every = rows * len(inputs)
    block = min(256, rows)
    return call(
        functools.partial(pass_kernel, len(inputs), shards, block),
        jax.ShapeDtypeStruct((shards, count // shards + extra, LANES), bf16),
        scratch=[
            pltpu.VMEM((2 * LANES, every), bf16),
            pltpu.VMEM((count, every), bf16),
            pltpu.VMEM((every, 2 * LANES), bf16),
            pltpu.VMEM((1, block), f32),
        ],
        in_specs=[whole(words)] + [whole(x) for x in inputs],
        name="em_pass",
    )(words, *inputs)


def update_kernel(shard, code_ref, *refs):
    messages, (new_ref, out_ref) = refs[:-2], refs[-2:]
    size = min(shard, LANES)
    per = shard // size
    total = jnp.zeros(messages[0].shape, f32)
    for ref in messages:
        total = total + ref[...].astype(f32)
    tail = total[shard:, :]
    counts_t = pad_rows(tail[0:per] + tail[per : 2 * per], LANES).T
    row = iota(tail.shape, 0)
    lane = iota((LANES, LANES), 1)
    norms = jnp.zeros(tail.shape, f32)
    for a in range(per):
        part = slice(a * size, (a + 1) * size)
        new = (total[part, :] + PRIOR * code_ref[part, :]) / (counts_t[0:size, a : a + 1] + PRIOR)
        new_ref[part, :] = new
        out_ref[part, :] = new.astype(bf16)
        norm = pad_rows(jnp.sum(new * new, axis=1, keepdims=True) * (-1.0 / SOFTNESS), LANES)
        columns = jnp.zeros((LANES, LANES), f32)
        for p, piece in enumerate(pieces(norm)):
            columns = jnp.where(lane == p, piece, columns)
        turned = columns.T
        for p in range(3):
            norms = jnp.where(row == p * per + a, turned[p : p + 1, :], norms)
    out_ref[shard:, :] = norms.astype(bf16)


def update(code, messages):
    shard = code.shape[0]
    return call(
        functools.partial(update_kernel, shard),
        (
            jax.ShapeDtypeStruct(code.shape, f32),
            jax.ShapeDtypeStruct(messages[0].shape, bf16),
        ),
        in_specs=[whole(code)] + [whole(m) for m in messages],
        name="update",
    )(code, *messages)


def finish_kernel(shards, where_ref, *refs):
    messages, out_ref = refs[:-1], refs[-1]
    spaces, words, _ = out_ref.shape
    shard = words // shards
    q, s = where_ref[0], where_ref[1]
    for t in range(spaces):
        space = lax.rem(s - t + spaces, spaces)
        for k in range(shards):
            start = pl.multiple_of((q ^ k) * shard, shard)
            out_ref[space, pl.ds(start, shard), :] = messages[t * shards + k][0:shard, :].astype(f32)


def finish(q, s, messages, shape, shards):
    return call(
        functools.partial(finish_kernel, shards),
        jax.ShapeDtypeStruct(shape, f32),
        in_specs=[whole(m) for m in messages],
        name="finish",
        prefetch=1,
    )(jnp.stack([q, s]).astype(i32), *messages)


def on_device(wide, samples, centroid_table, owner, slot, assign, codebook):
    spaces, words, sub_width = codebook.shape
    group_rows = assign.shape[0]
    cap = 2 * group_rows // wide
    shards = wide // spaces
    shard = words // shards
    per = max(1, shard // LANES)
    extra = -(-3 * per // 16) * 16
    me = lax.axis_index("wide")
    q, s = me // spaces, me % spaces

    def swap(x, k):
        return lax.ppermute(x, "wide", [(j, j ^ k) for j in range(wide)])

    def swap_shard(x, k):
        return lax.ppermute(x, "wide", [(j, j ^ (k * spaces)) for j in range(wide)])

    def turn(x, t):
        pairs = [(j, (j // spaces) * spaces + (j + t) % spaces) for j in range(wide)]
        return lax.ppermute(x, "wide", pairs)

    req, own, rank = lookup(assign, owner, slot, wide, cap)
    regrouped = lax.all_to_all(samples, "narrow", split_axis=1, concat_axis=0, tiled=True)
    asked = lax.all_to_all(req, "wide", 0, 0, tiled=True)
    chunks = pick(asked, centroid_table, spaces)
    moved = []
    for chunk in chunks:
        bufs = [lax.dynamic_index_in_dim(chunk, me, 0, keepdims=False)]
        for k in range(1, wide):
            bufs.append(swap(lax.dynamic_index_in_dim(chunk, me ^ k, 0, keepdims=False), k))
        moved.append(bufs)
    residuals, inputs = [], []
    for i in range(spaces):
        res, res_t = place(me, (s + 1 + i) % spaces, own, rank, regrouped, moved[i])
        residuals.append(res)
        inputs.append(res_t if i == spaces - 1 else turn(res_t, 1 + i))
    stacked = jnp.stack(residuals)
    residual = jnp.concatenate(
        [
            lax.dynamic_index_in_dim(stacked, (c - s - 1 + 2 * spaces) % spaces, 0, keepdims=False)
            for c in range(spaces)
        ],
        axis=1,
    )

    words_aug = first_words(s, codebook)
    mine = lax.dynamic_slice(codebook, (s, q * shard, 0), (1, shard, sub_width))[0]
    for iteration in range(ITERS):
        sums = em_pass(words_aug, inputs, shards, extra)
        parts = [lax.dynamic_index_in_dim(sums, q, 0, keepdims=False)]
        for k in range(1, shards):
            parts.append(swap_shard(lax.dynamic_index_in_dim(sums, q ^ k, 0, keepdims=False), k))
        mine, message = update(mine, parts)
        if iteration < ITERS - 1:
            got = [message] + [swap_shard(message, k) for k in range(1, shards)]
            words_aug = next_words(q, got, shard)
    message = message[0:shard]
    got = [message] + [swap_shard(message, k) for k in range(1, shards)]
    for t in range(1, spaces):
        got = got + [turn(m, t) for m in got[0:shards]]
    refined = finish(q, s, got, codebook.shape, shards)
    return (residual, refined)


def solution(mesh):
    wide = mesh.shape["wide"]
    return jax.shard_map(
        functools.partial(on_device, wide),
        mesh=mesh,
        in_specs=(
            P(("wide", "narrow"), None),
            P("wide", "narrow"),
            P(),
            P(),
            P("wide"),
            P("narrow", None, None),
        ),
        out_specs=(P("wide", "narrow"), P("narrow", None, None)),
        check_vma=False,
    )
```
